32 devices in a mesh: dp: 8 (over z, y), mp: 4 (over x, core).
Axes of the slice: x: 2, y: 2, z: 4, core: 2. Of those that a mesh axis runs over, the one named last changes fastest.
Arguments:
- q_grad: bfloat16 [8192, 8192], P('dp', 'mp'), may hold values from -200 to 200
- k_grad: bfloat16 [8192, 1024], P('dp', 'mp'), may hold values from -200 to 200
- v_grad: bfloat16 [8192, 1024], P('dp', 'mp'), may hold values from -200 to 200
- o_grad: bfloat16 [8192, 8192], P('dp', 'mp'), may hold values from -200 to 200
Outputs:
- q_step: bfloat16 [8192, 8192], P('dp', 'mp')
- k_step: bfloat16 [8192, 1024], P('dp', 'mp')
- v_step: bfloat16 [8192, 1024], P('dp', 'mp')
- o_step: bfloat16 [8192, 8192], P('dp', 'mp')
The draws below stay inside these ranges and needn't reach their ends.
All inputs are finite; a program needn't handle non-finite values.
Results may differ from the reference program's by a relative error of at most 0.001.
Values sent between devices are 32-bit elements; how exact they have to be, the bound alone decides.
No kernel may reach another device: no remote copies, remote signals or barrier semaphores. Data moves between devices by JAX's collectives and lax.ppermute only.
A program may use at most 64 MiB of HBM per device.

```python
import math
import jax
import jax.numpy as jnp
from jax import lax

D = 8192
ITERS = 3
QW = 8192
KVW = 1024
N_DP = 8


spike_gain = 30.0


def draw_matrix(key, row_count, col_count):
    subkeys = jax.random.split(key, 6)
    row_scale = jnp.exp(jax.random.uniform(subkeys[0], (row_count,), jnp.float32, math.log(0.3), math.log(3.0)))
    col_scale = jnp.exp(jax.random.uniform(subkeys[1], (col_count,), jnp.float32, math.log(0.3), math.log(3.0)))
    row_group = jax.random.randint(subkeys[2], (row_count,), 0, 10) < 5
    col_group = jax.random.randint(subkeys[3], (col_count,), 0, 10) < 4
    coupling_low = 0.02
    jitter = jnp.clip(jax.random.normal(subkeys[4], (row_count, col_count), jnp.float32), -4.0, 4.0)
    coupling = jnp.where(row_group[:, None] == col_group[None, :], 1.0, coupling_low).astype(jnp.float32)
    pairing = jax.random.permutation(subkeys[5], N_DP)
    row_block = jnp.arange(row_count) // (row_count // N_DP)
    col_block = jnp.arange(col_count) * N_DP // col_count
    raised = pairing[row_block][:, None] == col_block[None, :]
    raised_gain = jnp.where(raised, spike_gain, 1.0).astype(jnp.float32)
    entries = jitter * jnp.sqrt(coupling * raised_gain) * row_scale[:, None] * col_scale[None, :]
    return entries.astype(jnp.bfloat16)


def draw_q_grad(key, part):
    return draw_matrix(jax.random.fold_in(key, 11), D, QW)


def draw_k_grad(key, part):
    return draw_matrix(jax.random.fold_in(key, 12), D, KVW)


def draw_v_grad(key, part):
    return draw_matrix(jax.random.fold_in(key, 13), D, KVW)


def draw_o_grad(key, part):
    return draw_matrix(jax.random.fold_in(key, 14), QW, D)


def setup_inputs(seed: int = 0) -> dict:
    key_of = jax.random.split(jax.random.key(seed), 5)
    q_grad = draw_q_grad(jax.random.fold_in(key_of[4], 71), 0)
    k_grad = draw_k_grad(jax.random.fold_in(key_of[4], 71), 0)
    v_grad = draw_v_grad(jax.random.fold_in(key_of[4], 71), 0)
    o_grad = draw_o_grad(jax.random.fold_in(key_of[4], 71), 0)
    return {"q_grad": q_grad, "k_grad": k_grad, "v_grad": v_grad, "o_grad": o_grad}


EPSILON = 1e-06

def normalize(grad):
    matrix = grad.astype(jnp.float32)
    for sweep_index in range(ITERS):
        matrix = matrix * lax.rsqrt(lax.optimization_barrier(jnp.mean(matrix * matrix, axis=1, keepdims=True)) + EPSILON)
        matrix = matrix * lax.rsqrt(lax.optimization_barrier(jnp.mean(matrix * matrix, axis=0, keepdims=True)) + EPSILON)
    return matrix.astype(jnp.bfloat16)

def reference(q_grad, k_grad, v_grad, o_grad):
    return (normalize(q_grad), normalize(k_grad), normalize(v_grad), normalize(o_grad))
```

```python
import functools

import jax
import jax.numpy as jnp
from jax import lax
from jax.experimental import pallas as pl
from jax.experimental.pallas import tpu as pltpu
from jax.sharding import PartitionSpec as P

ITERS = 3
EPSILON = 1e-06
LANES = 128
DIRECT_LIMIT = 8

VM = pltpu.VMEM
WHOLE = pl.BlockSpec(memory_space=pltpu.VMEM)
OUTSIDE = pl.BlockSpec(memory_space=pl.ANY)
PARAMS = pltpu.CompilerParams(vmem_limit_bytes=16 << 20)


class Plan:
    def __init__(self, grads):
        self.count = len(grads)
        self.rows = grads[0].shape[0]
        self.cols = [grad.shape[1] for grad in grads]
        self.chunk = min(LANES, self.rows)
        self.chunks = self.rows // self.chunk
        self.tiles = [n // LANES for n in self.cols]
        self.row_inv = [1.0 / float(n * lax.axis_size("mp")) for n in self.cols]
        self.col_inv = 1.0 / float(self.rows * lax.axis_size("dp"))
        self.row_shape = (self.chunks * self.count, LANES)
        self.col_shape = (-(-sum(self.tiles) // 8) * 8, LANES)

    def first_tile(self, index):
        return sum(self.tiles[:index])


def lane_tile(t):
    return pl.ds(t * LANES, LANES)


def chunk_rows(plan, step):
    return pl.ds(pl.multiple_of(step * plan.chunk, plan.chunk), plan.chunk)


def put_row_sums(plan, step, sums, out_ref):
    lane = lax.broadcasted_iota(jnp.int32, (plan.chunk, LANES), 1)
    merged = jnp.zeros((plan.chunk, LANES), jnp.float32)
    for index in range(plan.count):
        merged = jnp.where(lane == index, sums[index] * plan.row_inv[index], merged)
    turned = merged.T
    out_ref[pl.ds(step * plan.count, plan.count), 0 : plan.chunk] = turned[0 : plan.count, :]


def row_columns(plan, step, ref):
    block = ref[pl.ds(step * plan.count, plan.count), 0 : plan.chunk]
    block = jnp.concatenate([block, jnp.zeros((8 - plan.count, plan.chunk), jnp.float32)], axis=0)
    turned = block.T
    return [
        jnp.broadcast_to(turned[:, index : index + 1], (plan.chunk, LANES))
        for index in range(plan.count)
    ]


def new_scale(parts, previous):
    total = parts[0]
    for part in parts[1:]:
        total = total + part
    if previous is None:
        return lax.rsqrt(total + EPSILON)
    return previous * lax.rsqrt(previous * previous * total + EPSILON)


def load_kernel(plan, *refs):
    count = plan.count
    sources, held, squares = refs[:count], refs[count : 2 * count], refs[2 * count : 3 * count]
    out_ref, sems = refs[3 * count], refs[3 * count + 1]

    def copy(step, index):
        rows = chunk_rows(plan, step)
        return pltpu.make_async_copy(
            sources[index].at[rows], held[index].at[rows], sems.at[step, index]
        )

    out_ref[...] = jnp.zeros(plan.row_shape, jnp.float32)
    for step in range(plan.chunks):
        for index in range(count):
            copy(step, index).start()

    def body(step, carry):
        rows = chunk_rows(plan, step)
        sums = []
        for index in range(count):
            copy(step, index).wait()
            total = None
            for t in range(plan.tiles[index]):
                wide = held[index][rows, lane_tile(t)].astype(jnp.float32)
                square = wide * wide
                squares[index][rows, lane_tile(t)] = square
                total = square if total is None else total + square
            sums.append(jnp.sum(total, axis=1, keepdims=True))
        put_row_sums(plan, step, sums, out_ref)
        return carry

    lax.fori_loop(0, plan.chunks, body, 0)


def row_kernel(plan, part_count, has_previous, *refs):
    count = plan.count
    squares, refs = refs[:count], refs[count:]
    parts, refs = refs[:part_count], refs[part_count:]
    previous = refs[0][...] if has_previous else None
    scale_ref, out_ref, weight = refs[1 if has_previous else 0 :]
    scale = new_scale(read_parts(parts), previous)
    scale_ref[...] = scale
    weight[...] = scale * scale
    out_ref[...] = jnp.zeros(plan.row_shape, jnp.float32)

    def body(step, carry):
        rows = chunk_rows(plan, step)
        sums = []
        for index in range(count):
            first = plan.first_tile(index)
            total = None
            for t in range(plan.tiles[index]):
                part = squares[index][rows, lane_tile(t)] * weight[first + t : first + t + 1, :]
                total = part if total is None else total + part
            sums.append(jnp.sum(total, axis=1, keepdims=True))
        put_row_sums(plan, step, sums, out_ref)
        return carry

    lax.fori_loop(0, plan.chunks, body, 0)


def read_parts(parts):
    values = []
    for part in parts:
        if len(part.shape) == 3:
            values.extend(part[slot] for slot in range(part.shape[0]))
        else:
            values.append(part[...])
    return values


def col_kernel(plan, part_count, has_previous, *refs):
    count = plan.count
    squares, refs = refs[:count], refs[count:]
    parts, refs = refs[:part_count], refs[part_count:]
    previous = refs[0][...] if has_previous else None
    scale_ref, out_ref, weight, sums = refs[1 if has_previous else 0 :]
    scale = new_scale(read_parts(parts), previous)
    scale_ref[...] = scale
    weight[...] = scale * scale
    sums[...] = jnp.zeros(sums.shape, jnp.float32)

    def body(step, carry):
        rows = chunk_rows(plan, step)
        weights = row_columns(plan, step, weight)
        for index in range(count):
            first = plan.first_tile(index)
            for t in range(plan.tiles[index]):
                part = squares[index][rows, lane_tile(t)] * weights[index]
                folded = jnp.sum(part.reshape(plan.chunk // 8, 8, LANES), axis=0)
                sums[first + t] = sums[first + t] + folded
        return carry

    lax.fori_loop(0, plan.chunks, body, 0)
    out_ref[...] = jnp.sum(sums[...], axis=1) * plan.col_inv


def last_kernel(plan, part_count, *refs):
    count = plan.count
    held, refs = refs[:count], refs[count:]
    parts, refs = refs[:part_count], refs[part_count:]
    previous, row_scale, refs = refs[0], refs[1], refs[2:]
    outs, refs = refs[:count], refs[count:]
    col_scale, stages, sems = refs[0], refs[1 : 1 + count], refs[1 + count]
    col_scale[...] = new_scale(read_parts(parts), previous[...])

    def copy(step, index):
        rows = chunk_rows(plan, step)
        return pltpu.make_async_copy(
            stages[index].at[rows], outs[index].at[rows], sems.at[step, index]
        )

    def body(step, carry):
        rows = chunk_rows(plan, step)
        weights = row_columns(plan, step, row_scale)
        for index in range(count):
            first = plan.first_tile(index)
            for t in range(plan.tiles[index]):
                wide = held[index][rows, lane_tile(t)].astype(jnp.float32)
                scaled = wide * weights[index] * col_scale[first + t : first + t + 1, :]
                stages[index][rows, lane_tile(t)] = scaled.astype(jnp.bfloat16)
            copy(step, index).start()
        return carry

    lax.fori_loop(0, plan.chunks, body, 0)
    for step in range(plan.chunks):
        for index in range(count):
            copy(step, index).wait()


def exchange_rows(part):
    size = lax.axis_size("mp")
    if size > DIRECT_LIMIT or size & (size - 1):
        return [lax.psum(part, "mp")]
    parts = [part]
    for offset in range(1, size):
        pairs = [(index, index ^ offset) for index in range(size)]
        parts.append(lax.ppermute(part, "mp", pairs))
    return parts


def exchange_cols(part):
    size = lax.axis_size("dp")
    if size > DIRECT_LIMIT:
        return [lax.psum(part, "dp")]
    copies = jnp.broadcast_to(part[None], (size,) + part.shape)
    return [lax.all_to_all(copies, "dp", 0, 0)]


def shards(q_grad, k_grad, v_grad, o_grad):
    grads = (q_grad, k_grad, v_grad, o_grad)
    plan = Plan(grads)
    count = plan.count
    f32 = jnp.float32
    row_out = VM(plan.row_shape, f32)
    col_out = VM(plan.col_shape, f32)

    loaded = pl.pallas_call(
        functools.partial(load_kernel, plan),
        in_specs=[OUTSIDE] * count,
        out_specs=[WHOLE] * (2 * count + 1),
        out_shape=[VM(grad.shape, grad.dtype) for grad in grads]
        + [VM(grad.shape, f32) for grad in grads]
        + [row_out],
        scratch_shapes=[pltpu.SemaphoreType.DMA((plan.chunks, count))],
        compiler_params=PARAMS,
        name="load",
    )(*grads)
    held, squares, row_part = loaded[:count], loaded[count : 2 * count], loaded[2 * count]

    row_scale = col_scale = None
    for sweep in range(ITERS):
        parts = exchange_rows(row_part)
        previous = [] if row_scale is None else [row_scale]
        row_scale, col_part = pl.pallas_call(
            functools.partial(col_kernel, plan, len(parts), bool(previous)),
            in_specs=[WHOLE] * (count + len(parts) + len(previous)),
            out_specs=[WHOLE] * 2,
            out_shape=[row_out, col_out],
            scratch_shapes=[
                VM(plan.row_shape, f32),
                VM((plan.col_shape[0], 8, LANES), f32),
            ],
            compiler_params=PARAMS,
            name=f"col{sweep}",
        )(*squares, *parts, *previous)
        parts = exchange_cols(col_part)
        previous = [] if col_scale is None else [col_scale]
        if sweep + 1 == ITERS:
            break
        col_scale, row_part = pl.pallas_call(
            functools.partial(row_kernel, plan, len(parts), bool(previous)),
            in_specs=[WHOLE] * (count + len(parts) + len(previous)),
            out_specs=[WHOLE] * 2,
            out_shape=[col_out, row_out],
            scratch_shapes=[VM(plan.col_shape, f32)],
            compiler_params=PARAMS,
            name=f"row{sweep}",
        )(*squares, *parts, *previous)

    return tuple(
        pl.pallas_call(
            functools.partial(last_kernel, plan, len(parts)),
            in_specs=[WHOLE] * (count + len(parts) + 2),
            out_specs=[OUTSIDE] * count,
            out_shape=[jax.ShapeDtypeStruct(grad.shape, grad.dtype) for grad in grads],
            scratch_shapes=[VM(plan.col_shape, f32)]
            + [VM(grad.shape, grad.dtype) for grad in grads]
            + [pltpu.SemaphoreType.DMA((plan.chunks, count))],
            compiler_params=PARAMS,
            name="last",
        )(*held, *parts, col_scale, row_scale)
    )


def solution(mesh):
    return jax.shard_map(
        shards,
        mesh=mesh,
        in_specs=(P("dp", "mp"), P("dp", "mp"), P("dp", "mp"), P("dp", "mp")),
        out_specs=(P("dp", "mp"), P("dp", "mp"), P("dp", "mp"), P("dp", "mp")),
        check_vma=False,
    )
```

```python
import functools

import jax
import jax.numpy as jnp
from jax import lax
from jax.experimental import pallas as pl
from jax.experimental.pallas import tpu as pltpu
from jax.sharding import PartitionSpec as P

ITERS = 3
EPSILON = 1e-06
LANES = 128
DIRECT_LIMIT = 8
UNROLL = 4

VM = pltpu.VMEM
WHOLE = pl.BlockSpec(memory_space=pltpu.VMEM)
OUTSIDE = pl.BlockSpec(memory_space=pltpu.HBM)
PARAMS = pltpu.CompilerParams(vmem_limit_bytes=16 << 20)


class Plan:
    def __init__(self, grads):
        self.count = len(grads)
        self.rows = grads[0].shape[0]
        self.cols = [grad.shape[1] for grad in grads]
        self.chunk = min(LANES, self.rows)
        self.chunks = self.rows // self.chunk
        self.unroll = min(UNROLL, self.chunks)
        self.tiles = [n // LANES for n in self.cols]
        self.group = [2 if t % 2 == 0 else 1 for t in self.tiles]
        self.row_inv = [1.0 / float(n * lax.axis_size("mp")) for n in self.cols]
        self.col_inv = 1.0 / float(self.rows * lax.axis_size("dp"))
        self.row_shape = (self.chunks * self.count, LANES)
        self.col_shape = (-(-sum(self.tiles) // 8) * 8, LANES)

    def first_tile(self, index):
        return sum(self.tiles[:index])


def lane_tile(t):
    return pl.ds(t * LANES, LANES)


def chunk_rows(plan, step):
    return pl.ds(pl.multiple_of(step * plan.chunk, plan.chunk), plan.chunk)


def put_row_sums(plan, step, sums, out_ref):
    lane = lax.broadcasted_iota(jnp.int32, (plan.chunk, LANES), 1)
    merged = jnp.zeros((plan.chunk, LANES), jnp.float32)
    for index in range(plan.count):
        merged = jnp.where(lane == index, sums[index] * plan.row_inv[index], merged)
    turned = merged.T
    out_ref[pl.ds(step * plan.count, plan.count), 0 : plan.chunk] = turned[0 : plan.count, :]


def row_columns(plan, step, ref):
    block = ref[pl.ds(step * plan.count, plan.count), 0 : plan.chunk]
    block = jnp.concatenate([block, jnp.zeros((8 - plan.count, plan.chunk), jnp.float32)], axis=0)
    turned = block.T
    return [
        jnp.broadcast_to(turned[:, index : index + 1], (plan.chunk, LANES))
        for index in range(plan.count)
    ]


def new_scale(parts, previous):
    total = parts[0]
    for part in parts[1:]:
        total = total + part
    if previous is None:
        return lax.rsqrt(total + EPSILON)
    return previous * lax.rsqrt(previous * previous * total + EPSILON)


def load_kernel(plan, *refs):
    count = plan.count
    sources, held, squares = refs[:count], refs[count : 2 * count], refs[2 * count : 3 * count]
    out_ref, sems = refs[3 * count], refs[3 * count + 1]

    def copy(step, index):
        rows = chunk_rows(plan, step)
        return pltpu.make_async_copy(
            sources[index].at[rows], held[index].at[rows], sems.at[step, index]
        )

    out_ref[...] = jnp.zeros(plan.row_shape, jnp.float32)
    for step in range(plan.chunks):
        for index in range(count):
            copy(step, index).start()

    def body(step, carry):
        rows = chunk_rows(plan, step)
        sums = []
        for index in range(count):
            copy(step, index).wait()
        for index in range(count):
            total = None
            group = plan.group[index]
            for t in range(0, plan.tiles[index], group):
                span = pl.ds(t * LANES, group * LANES)
                wide = held[index][rows, span].astype(jnp.float32)
                square = wide * wide
                squares[index][rows, span] = square
                for k in range(group):
                    part = square[:, k * LANES : (k + 1) * LANES]
                    total = part if total is None else total + part
            sums.append(jnp.sum(total, axis=1, keepdims=True))
        put_row_sums(plan, step, sums, out_ref)
        return carry

    lax.fori_loop(0, plan.chunks, body, 0)


def row_kernel(plan, part_count, has_previous, *refs):
    count = plan.count
    squares, refs = refs[:count], refs[count:]
    parts, refs = refs[:part_count], refs[part_count:]
    previous = refs[0][...] if has_previous else None
    scale_ref, out_ref, weight = refs[1 if has_previous else 0 :]
    scale = new_scale(read_parts(parts), previous)
    scale_ref[...] = scale
    weight[...] = scale * scale
    out_ref[...] = jnp.zeros(plan.row_shape, jnp.float32)

    def body(step, carry):
        rows = chunk_rows(plan, step)
        sums = []
        for index in range(count):
            first = plan.first_tile(index)
            total = None
            for t in range(plan.tiles[index]):
                part = squares[index][rows, lane_tile(t)] * weight[first + t : first + t + 1, :]
                total = part if total is None else total + part
            sums.append(jnp.sum(total, axis=1, keepdims=True))
        put_row_sums(plan, step, sums, out_ref)
        return carry

    lax.fori_loop(0, plan.chunks, body, 0, unroll=plan.unroll)


def read_parts(parts):
    values = []
    for part in parts:
        if len(part.shape) == 3:
            values.extend(part[slot] for slot in range(part.shape[0]))
        else:
            values.append(part[...])
    return values


def col_kernel(plan, part_count, has_previous, *refs):
    count = plan.count
    squares, refs = refs[:count], refs[count:]
    parts, refs = refs[:part_count], refs[part_count:]
    previous = refs[0][...] if has_previous else None
    scale_ref, out_ref, weight, sums = refs[1 if has_previous else 0 :]
    scale = new_scale(read_parts(parts), previous)
    scale_ref[...] = scale
    weight[...] = scale * scale
    sums[...] = jnp.zeros(sums.shape, jnp.float32)

    def body(step, carry):
        rows = chunk_rows(plan, step)
        weights = row_columns(plan, step, weight)
        for index in range(count):
            first = plan.first_tile(index)
            for t in range(plan.tiles[index]):
                part = squares[index][rows, lane_tile(t)] * weights[index]
                folded = jnp.sum(part.reshape(plan.chunk // 8, 8, LANES), axis=0)
                sums[first + t] = sums[first + t] + folded
        return carry

    lax.fori_loop(0, plan.chunks, body, 0, unroll=plan.unroll)
    out_ref[...] = jnp.sum(sums[...], axis=1) * plan.col_inv


def last_kernel(plan, part_count, *refs):
    count = plan.count
    held, refs = refs[:count], refs[count:]
    parts, refs = refs[:part_count], refs[part_count:]
    previous, row_scale, refs = refs[0], refs[1], refs[2:]
    outs, refs = refs[:count], refs[count:]
    col_scale, stages, sems = refs[0], refs[1 : 1 + count], refs[1 + count]
    col_scale[...] = new_scale(read_parts(parts), previous[...])

    def copy(step, index):
        rows = chunk_rows(plan, step)
        return pltpu.make_async_copy(
            stages[index].at[rows], outs[index].at[rows], sems.at[step, index]
        )

    def body(step, carry):
        rows = chunk_rows(plan, step)
        weights = row_columns(plan, step, row_scale)
        for index in range(count):
            first = plan.first_tile(index)
            group = plan.group[index]
            weight = jnp.concatenate([weights[index]] * group, axis=1)
            for t in range(0, plan.tiles[index], group):
                span = pl.ds(t * LANES, group * LANES)
                cols = [col_scale[first + t + k : first + t + k + 1, :] for k in range(group)]
                wide = held[index][rows, span].astype(jnp.float32)
                scaled = wide * weight * jnp.concatenate(cols, axis=1)
                stages[index][rows, span] = scaled.astype(stages[index].dtype)
        for index in range(count):
            copy(step, index).start()
        return carry

    lax.fori_loop(0, plan.chunks, body, 0, unroll=2)
    for step in range(plan.chunks):
        for index in range(count):
            copy(step, index).wait()


def exchange_rows(part):
    size = lax.axis_size("mp")
    if size > DIRECT_LIMIT or size & (size - 1):
        return [lax.psum(part, "mp")]
    parts = [part]
    for offset in range(1, size):
        pairs = [(index, index ^ offset) for index in range(size)]
        parts.append(lax.ppermute(part, "mp", pairs))
    return parts


def exchange_cols(part):
    size = lax.axis_size("dp")
    if size > DIRECT_LIMIT:
        return [lax.psum(part, "dp")]
    copies = jnp.broadcast_to(part[None], (size,) + part.shape)
    return [lax.all_to_all(copies, "dp", 0, 0)]


def shards(q_grad, k_grad, v_grad, o_grad):
    grads = (q_grad, k_grad, v_grad, o_grad)
    plan = Plan(grads)
    count = plan.count
    f32 = jnp.float32
    row_out = VM(plan.row_shape, f32)
    col_out = VM(plan.col_shape, f32)

    loaded = pl.pallas_call(
        functools.partial(load_kernel, plan),
        in_specs=[OUTSIDE] * count,
        out_specs=[WHOLE] * (2 * count + 1),
        out_shape=[VM(grad.shape, grad.dtype) for grad in grads]
        + [VM(grad.shape, f32) for grad in grads]
        + [row_out],
        scratch_shapes=[pltpu.SemaphoreType.DMA((plan.chunks, count))],
        compiler_params=PARAMS,
        name="load",
    )(*[pltpu.with_memory_space_constraint(grad, pltpu.HBM) for grad in grads])
    held, squares, row_part = loaded[:count], loaded[count : 2 * count], loaded[2 * count]

    row_scale = col_scale = None
    for sweep in range(ITERS):
        parts = exchange_rows(row_part)
        previous = [] if row_scale is None else [row_scale]
        row_scale, col_part = pl.pallas_call(
            functools.partial(col_kernel, plan, len(parts), bool(previous)),
            in_specs=[WHOLE] * (count + len(parts) + len(previous)),
            out_specs=[WHOLE] * 2,
            out_shape=[row_out, col_out],
            scratch_shapes=[
                VM(plan.row_shape, f32),
                VM((plan.col_shape[0], 8, LANES), f32),
            ],
            compiler_params=PARAMS,
            name=f"col{sweep}",
        )(*squares, *parts, *previous)
        parts = exchange_cols(col_part)
        previous = [] if col_scale is None else [col_scale]
        if sweep + 1 == ITERS:
            break
        col_scale, row_part = pl.pallas_call(
            functools.partial(row_kernel, plan, len(parts), bool(previous)),
            in_specs=[WHOLE] * (count + len(parts) + len(previous)),
            out_specs=[WHOLE] * 2,
            out_shape=[col_out, row_out],
            scratch_shapes=[VM(plan.col_shape, f32)],
            compiler_params=PARAMS,
            name=f"row{sweep}",
        )(*squares, *parts, *previous)

    return tuple(
        pl.pallas_call(
            functools.partial(last_kernel, plan, len(parts)),
            in_specs=[WHOLE] * (count + len(parts) + 2),
            out_specs=[OUTSIDE] * count,
            out_shape=[jax.ShapeDtypeStruct(grad.shape, grad.dtype) for grad in grads],
            scratch_shapes=[VM(plan.col_shape, f32)]
            + [VM(grad.shape, grad.dtype) for grad in grads]
            + [pltpu.SemaphoreType.DMA((plan.chunks, count))],
            compiler_params=PARAMS,
            name="last",
        )(*held, *parts, col_scale, row_scale)
    )


def solution(mesh):
    return jax.shard_map(
        shards,
        mesh=mesh,
        in_specs=(P("dp", "mp"), P("dp", "mp"), P("dp", "mp"), P("dp", "mp")),
        out_specs=(P("dp", "mp"), P("dp", "mp"), P("dp", "mp"), P("dp", "mp")),
        check_vma=False,
    )
```

```python
import functools

import jax
import jax.numpy as jnp
from jax import lax
from jax.experimental import pallas as pl
from jax.experimental.pallas import tpu as pltpu
from jax.sharding import PartitionSpec as P

ITERS = 3
EPSILON = 1e-06
LANES = 128
DIRECT_LIMIT = 8
UNROLL = 4

VM = pltpu.VMEM
WHOLE = pl.BlockSpec(memory_space=pltpu.VMEM)
OUTSIDE = pl.BlockSpec(memory_space=pltpu.HBM)
PARAMS = pltpu.CompilerParams(vmem_limit_bytes=16 << 20)


class Plan:
    def __init__(self, grads):
        self.count = len(grads)
        self.rows = grads[0].shape[0]
        self.cols = [grad.shape[1] for grad in grads]
        self.chunk = min(LANES, self.rows)
        self.chunks = self.rows // self.chunk
        self.unroll = min(UNROLL, self.chunks)
        self.tiles = [n // LANES for n in self.cols]
        self.group = [2 if t % 2 == 0 else 1 for t in self.tiles]
        self.starts = [sum(self.cols[:index]) for index in range(self.count)]
        self.wide = (self.rows, sum(self.cols))
        self.row_inv = [1.0 / float(n * lax.axis_size("mp")) for n in self.cols]
        self.col_inv = 1.0 / float(self.rows * lax.axis_size("dp"))
        self.row_shape = (self.chunks * self.count, LANES)
        self.col_shape = (-(-sum(self.tiles) // 8) * 8, LANES)

    def span(self, index, t):
        return pl.ds(self.starts[index] + t * LANES, self.group[index] * LANES)

    def first_tile(self, index):
        return sum(self.tiles[:index])


def lane_tile(t):
    return pl.ds(t * LANES, LANES)


def chunk_rows(plan, step):
    return pl.ds(pl.multiple_of(step * plan.chunk, plan.chunk), plan.chunk)


def put_row_sums(plan, step, sums, out_ref):
    lane = lax.broadcasted_iota(jnp.int32, (plan.chunk, LANES), 1)
    merged = jnp.zeros((plan.chunk, LANES), jnp.float32)
    for index in range(plan.count):
        merged = jnp.where(lane == index, sums[index] * plan.row_inv[index], merged)
    turned = merged.T
    out_ref[pl.ds(step * plan.count, plan.count), 0 : plan.chunk] = turned[0 : plan.count, :]


def row_columns(plan, step, ref):
    block = ref[pl.ds(step * plan.count, plan.count), 0 : plan.chunk]
    block = jnp.concatenate([block, jnp.zeros((8 - plan.count, plan.chunk), jnp.float32)], axis=0)
    turned = block.T
    return [
        jnp.broadcast_to(turned[:, index : index + 1], (plan.chunk, LANES))
        for index in range(plan.count)
    ]


def new_scale(parts, previous):
    total = parts[0]
    for part in parts[1:]:
        total = total + part
    if previous is None:
        return lax.rsqrt(total + EPSILON)
    return previous * lax.rsqrt(previous * previous * total + EPSILON)


def load_kernel(plan, *refs):
    count = plan.count
    sources, held, squares = refs[:count], refs[count], refs[count + 1 : 2 * count + 1]
    out_ref, sems = refs[2 * count + 1 :]

    def copy(step, index):
        rows = chunk_rows(plan, step)
        cols = pl.ds(plan.starts[index], plan.cols[index])
        return pltpu.make_async_copy(
            sources[index].at[rows], held.at[rows, cols], sems.at[step]
        )

    out_ref[...] = jnp.zeros(plan.row_shape, jnp.float32)
    for step in range(plan.chunks):
        for index in range(count):
            copy(step, index).start()

    def body(step, carry):
        rows = chunk_rows(plan, step)
        sums = []
        arrived = held.at[rows]
        pltpu.make_async_copy(arrived, arrived, sems.at[step]).wait()
        for index in range(count):
            total = None
            group = plan.group[index]
            for t in range(0, plan.tiles[index], group):
                span = pl.ds(t * LANES, group * LANES)
                wide = held[rows, plan.span(index, t)].astype(jnp.float32)
                square = wide * wide
                squares[index][rows, span] = square
                for k in range(group):
                    part = square[:, k * LANES : (k + 1) * LANES]
                    total = part if total is None else total + part
            sums.append(jnp.sum(total, axis=1, keepdims=True))
        put_row_sums(plan, step, sums, out_ref)
        return carry

    lax.fori_loop(0, plan.chunks, body, 0)


def row_kernel(plan, part_count, has_previous, *refs):
    count = plan.count
    squares, refs = refs[:count], refs[count:]
    parts, refs = refs[:part_count], refs[part_count:]
    previous = refs[0][...] if has_previous else None
    scale_ref, out_ref, weight = refs[1 if has_previous else 0 :]
    scale = new_scale(read_parts(parts), previous)
    scale_ref[...] = scale
    weight[...] = scale * scale
    out_ref[...] = jnp.zeros(plan.row_shape, jnp.float32)

    def body(step, carry):
        rows = chunk_rows(plan, step)
        sums = []
        for index in range(count):
            first = plan.first_tile(index)
            total = None
            for t in range(plan.tiles[index]):
                part = squares[index][rows, lane_tile(t)] * weight[first + t : first + t + 1, :]
                total = part if total is None else total + part
            sums.append(jnp.sum(total, axis=1, keepdims=True))
        put_row_sums(plan, step, sums, out_ref)
        return carry

    lax.fori_loop(0, plan.chunks, body, 0, unroll=plan.unroll)


def read_parts(parts):
    values = []
    for part in parts:
        if len(part.shape) == 3:
            values.extend(part[slot] for slot in range(part.shape[0]))
        else:
            values.append(part[...])
    return values


def col_kernel(plan, part_count, has_previous, *refs):
    count = plan.count
    squares, refs = refs[:count], refs[count:]
    parts, refs = refs[:part_count], refs[part_count:]
    previous = refs[0][...] if has_previous else None
    scale_ref, out_ref, weight, sums = refs[1 if has_previous else 0 :]
    scale = new_scale(read_parts(parts), previous)
    scale_ref[...] = scale
    weight[...] = scale * scale
    sums[...] = jnp.zeros(sums.shape, jnp.float32)

    def body(step, carry):
        rows = chunk_rows(plan, step)
        weights = row_columns(plan, step, weight)
        for index in range(count):
            first = plan.first_tile(index)
            for t in range(plan.tiles[index]):
                part = squares[index][rows, lane_tile(t)] * weights[index]
                folded = jnp.sum(part.reshape(plan.chunk // 8, 8, LANES), axis=0)
                sums[first + t] = sums[first + t] + folded
        return carry

    lax.fori_loop(0, plan.chunks, body, 0, unroll=plan.unroll)
    out_ref[...] = jnp.sum(sums[...], axis=1) * plan.col_inv


def scale_kernel(plan, held, row_scale, out_ref):
    def body(step, carry):
        rows = chunk_rows(plan, step)
        weights = row_columns(plan, step, row_scale)
        for index in range(plan.count):
            weight = jnp.concatenate([weights[index]] * plan.group[index], axis=1)
            for t in range(0, plan.tiles[index], plan.group[index]):
                span = plan.span(index, t)
                out_ref[rows, span] = held[rows, span].astype(jnp.float32) * weight
        return carry

    lax.fori_loop(0, plan.chunks, body, 0, unroll=min(2, plan.chunks))


def last_kernel(plan, part_count, *refs):
    count = plan.count
    scaled, refs = refs[0], refs[1:]
    parts, refs = refs[:part_count], refs[part_count:]
    previous, refs = refs[0], refs[1:]
    outs, refs = refs[:count], refs[count:]
    col_scale, stage, sems = refs
    col_scale[...] = new_scale(read_parts(parts), previous[...])

    def copy(step, index):
        rows = chunk_rows(plan, step)
        cols = pl.ds(plan.starts[index], plan.cols[index])
        return pltpu.make_async_copy(
            stage.at[rows, cols], outs[index].at[rows], sems.at[step]
        )

    def body(step, carry):
        rows = chunk_rows(plan, step)
        for index in range(count):
            first = plan.first_tile(index)
            group = plan.group[index]
            for t in range(0, plan.tiles[index], group):
                span = plan.span(index, t)
                cols = [col_scale[first + t + k : first + t + k + 1, :] for k in range(group)]
                value = scaled[rows, span] * jnp.concatenate(cols, axis=1)
                stage[rows, span] = value.astype(stage.dtype)
        for index in range(count):
            copy(step, index).start()
        return carry

    lax.fori_loop(0, plan.chunks, body, 0, unroll=2)
    for step in range(plan.chunks):
        sent = stage.at[chunk_rows(plan, step)]
        pltpu.make_async_copy(sent, sent, sems.at[step]).wait()


def exchange_rows(part):
    size = lax.axis_size("mp")
    if size > DIRECT_LIMIT or size & (size - 1):
        return [lax.psum(part, "mp")]
    parts = [part]
    for offset in range(1, size):
        pairs = [(index, index ^ offset) for index in range(size)]
        parts.append(lax.ppermute(part, "mp", pairs))
    return parts


def exchange_cols(part):
    size = lax.axis_size("dp")
    if size > DIRECT_LIMIT or size & (size - 1):
        return [lax.psum(part, "dp")]
    if size == 1:
        return [part]
    pair = part + lax.ppermute(part, "dp", [(index, index ^ 1) for index in range(size)])
    parts = [pair]
    for offset in range(2, size, 2):
        parts.append(lax.ppermute(pair, "dp", [(index, index ^ offset) for index in range(size)]))
    return parts


def shards(q_grad, k_grad, v_grad, o_grad):
    grads = (q_grad, k_grad, v_grad, o_grad)
    plan = Plan(grads)
    count = plan.count
    f32 = jnp.float32
    row_out = VM(plan.row_shape, f32)
    col_out = VM(plan.col_shape, f32)

    loaded = pl.pallas_call(
        functools.partial(load_kernel, plan),
        in_specs=[OUTSIDE] * count,
        out_specs=[WHOLE] * (count + 2),
        out_shape=[VM(plan.wide, grads[0].dtype)]
        + [VM(grad.shape, f32) for grad in grads]
        + [row_out],
        scratch_shapes=[pltpu.SemaphoreType.DMA((plan.chunks,))],
        compiler_params=PARAMS,
        name="load",
    )(*[pltpu.with_memory_space_constraint(grad, pltpu.HBM) for grad in grads])
    held, squares, row_part = loaded[0], loaded[1 : 1 + count], loaded[1 + count]

    row_scale = col_scale = None
    for sweep in range(ITERS):
        parts = exchange_rows(row_part)
        previous = [] if row_scale is None else [row_scale]
        row_scale, col_part = pl.pallas_call(
            functools.partial(col_kernel, plan, len(parts), bool(previous)),
            in_specs=[WHOLE] * (count + len(parts) + len(previous)),
            out_specs=[WHOLE] * 2,
            out_shape=[row_out, col_out],
            scratch_shapes=[
                VM(plan.row_shape, f32),
                VM((plan.col_shape[0], 8, LANES), f32),
            ],
            compiler_params=PARAMS,
            name=f"col{sweep}",
        )(*squares, *parts, *previous)
        parts = exchange_cols(col_part)
        previous = [] if col_scale is None else [col_scale]
        if sweep + 1 == ITERS:
            break
        col_scale, row_part = pl.pallas_call(
            functools.partial(row_kernel, plan, len(parts), bool(previous)),
            in_specs=[WHOLE] * (count + len(parts) + len(previous)),
            out_specs=[WHOLE] * 2,
            out_shape=[col_out, row_out],
            scratch_shapes=[VM(plan.col_shape, f32)],
            compiler_params=PARAMS,
            name=f"row{sweep}",
        )(*squares, *parts, *previous)

    size = plan.wide[0] * plan.wide[1]
    scaled = pl.pallas_call(
        functools.partial(scale_kernel, plan),
        in_specs=[WHOLE] * 2,
        out_specs=WHOLE,
        out_shape=VM(plan.wide, f32),
        compiler_params=PARAMS,
        cost_estimate=pl.CostEstimate(flops=2 * size, bytes_accessed=6 * size, transcendentals=0),
        name="scale",
    )(held, row_scale)
    return tuple(
        pl.pallas_call(
            functools.partial(last_kernel, plan, len(parts)),
            in_specs=[WHOLE] * (len(parts) + 2),
            out_specs=[OUTSIDE] * count,
            out_shape=[jax.ShapeDtypeStruct(grad.shape, grad.dtype) for grad in grads],
            scratch_shapes=[VM(plan.col_shape, f32)]
            + [VM(plan.wide, grads[0].dtype)]
            + [pltpu.SemaphoreType.DMA((plan.chunks,))],
            compiler_params=PARAMS,
            name="last",
        )(scaled, *parts, col_scale)
    )


def solution(mesh):
    return jax.shard_map(
        shards,
        mesh=mesh,
        in_specs=(P("dp", "mp"), P("dp", "mp"), P("dp", "mp"), P("dp", "mp")),
        out_specs=(P("dp", "mp"), P("dp", "mp"), P("dp", "mp"), P("dp", "mp")),
        check_vma=False,
    )
```

```python
import functools

import jax
import jax.numpy as jnp
from jax import lax
from jax.experimental import pallas as pl
from jax.experimental.pallas import tpu as pltpu
from jax.sharding import PartitionSpec as P

ITERS = 3
EPSILON = 1e-06
LANES = 128
DIRECT_LIMIT = 8
UNROLL = 4
ROW_UNROLL = 4

VM = pltpu.VMEM
WHOLE = pl.BlockSpec(memory_space=pltpu.VMEM)
OUTSIDE = pl.BlockSpec(memory_space=pltpu.HBM)
PARAMS = pltpu.CompilerParams(vmem_limit_bytes=16 << 20)


class Plan:
    def __init__(self, grads):
        self.count = len(grads)
        self.rows = grads[0].shape[0]
        self.cols = [grad.shape[1] for grad in grads]
        self.chunk = min(LANES, self.rows)
        self.chunks = self.rows // self.chunk
        self.unroll = min(UNROLL, self.chunks)
        self.tiles = [n // LANES for n in self.cols]
        self.group = [2 if t % 2 == 0 else 1 for t in self.tiles]
        self.starts = [sum(self.cols[:index]) for index in range(self.count)]
        self.wide = (self.rows, sum(self.cols))
        self.row_inv = [1.0 / float(n * lax.axis_size("mp")) for n in self.cols]
        self.col_inv = 1.0 / float(self.rows * lax.axis_size("dp"))
        self.row_shape = (self.chunks * self.count, LANES)
        self.col_shape = (-(-sum(self.tiles) // 8) * 8, LANES)

    def span(self, index, t):
        return pl.ds(self.starts[index] + t * LANES, self.group[index] * LANES)

    def first_tile(self, index):
        return sum(self.tiles[:index])


def lane_tile(t):
    return pl.ds(t * LANES, LANES)


def chunk_rows(plan, step):
    return pl.ds(pl.multiple_of(step * plan.chunk, plan.chunk), plan.chunk)


def put_row_sums(plan, step, sums, out_ref):
    lane = lax.broadcasted_iota(jnp.int32, sums[0].shape[:1] + (LANES,), 1)
    merged = jnp.broadcast_to(sums[0], lane.shape)
    for index in range(1, plan.count):
        merged = jnp.where(lane == index, sums[index], merged)
    put_merged(plan, step, merged, out_ref)


def put_merged(plan, step, merged, out_ref):
    turned = merged.T[0 : plan.count, :]
    place = lax.broadcasted_iota(jnp.int32, turned.shape, 0)
    scale = jnp.full(turned.shape, plan.row_inv[0], jnp.float32)
    for index in range(1, plan.count):
        scale = jnp.where(place == index, plan.row_inv[index], scale)
    out_ref[pl.ds(step * plan.count, plan.count), 0 : plan.chunk] = turned * scale


def row_columns(plan, step, ref):
    block = ref[pl.ds(step * plan.count, plan.count), 0 : plan.chunk]
    block = jnp.concatenate([block, jnp.zeros((8 - plan.count, plan.chunk), jnp.float32)], axis=0)
    turned = block.T
    return [
        jnp.broadcast_to(turned[:, index : index + 1], (plan.chunk, LANES))
        for index in range(plan.count)
    ]


def new_scale(parts, previous):
    total = parts[0]
    for part in parts[1:]:
        total = total + part
    if previous is None:
        return lax.rsqrt(total + EPSILON)
    return previous * lax.rsqrt(previous * previous * total + EPSILON)


def load_kernel(plan, *refs):
    count = plan.count
    sources, held, squares = refs[:count], refs[count], refs[count + 1 : 2 * count + 1]
    out_ref, sems = refs[2 * count + 1 :]

    def copy(step, index):
        rows = chunk_rows(plan, step)
        cols = pl.ds(plan.starts[index], plan.cols[index])
        return pltpu.make_async_copy(
            sources[index].at[rows], held.at[rows, cols], sems.at[step]
        )

    out_ref[...] = jnp.zeros(plan.row_shape, jnp.float32)
    for step in range(plan.chunks):
        for index in range(count):
            copy(step, index).start()

    def body(step, carry):
        rows = chunk_rows(plan, step)
        sums = []
        arrived = held.at[rows]
        pltpu.make_async_copy(arrived, arrived, sems.at[step]).wait()
        for index in range(count):
            total = None
            group = plan.group[index]
            for t in range(0, plan.tiles[index], group):
                span = pl.ds(t * LANES, group * LANES)
                wide = held[rows, plan.span(index, t)].astype(jnp.float32)
                square = wide * wide
                squares[index][rows, span] = square
                for k in range(group):
                    part = square[:, k * LANES : (k + 1) * LANES]
                    total = part if total is None else total + part
            sums.append(jnp.sum(total, axis=1, keepdims=True))
        put_row_sums(plan, step, sums, out_ref)
        return carry

    lax.fori_loop(0, plan.chunks, body, 0)


def row_kernel(plan, part_count, has_previous, *refs):
    count = plan.count
    squares, refs = refs[:count], refs[count:]
    parts, refs = refs[:part_count], refs[part_count:]
    previous = refs[0][...] if has_previous else None
    scale_ref, out_ref, weight = refs[1 if has_previous else 0 :]
    scale = new_scale(read_parts(parts), previous)
    scale_ref[...] = scale
    weight[...] = scale * scale
    out_ref[...] = jnp.zeros(plan.row_shape, jnp.float32)

    weights = [jnp.broadcast_to(weight[t : t + 1, :], (8, LANES)) for t in range(sum(plan.tiles))]

    def body(step, carry):
        lane = lax.broadcasted_iota(jnp.int32, (8, LANES), 1)
        merged = []
        for group in range(plan.chunk // 8):
            rows = pl.ds(pl.multiple_of(step * plan.chunk + group * 8, 8), 8)
            line = None
            for index in range(count):
                first = plan.first_tile(index)
                total = None
                for t in range(plan.tiles[index]):
                    part = squares[index][rows, lane_tile(t)] * weights[first + t]
                    total = part if total is None else total + part
                total = jnp.broadcast_to(jnp.sum(total, axis=1, keepdims=True), (8, LANES))
                line = total if line is None else jnp.where(lane == index, total, line)
            merged.append(line)
        put_merged(plan, step, jnp.concatenate(merged, axis=0), out_ref)
        return carry

    lax.fori_loop(0, plan.chunks, body, 0, unroll=min(ROW_UNROLL, plan.chunks))


def read_parts(parts):
    values = []
    for part in parts:
        if len(part.shape) == 3:
            values.extend(part[slot] for slot in range(part.shape[0]))
        else:
            values.append(part[...])
    return values


def col_kernel(plan, part_count, has_previous, *refs):
    count = plan.count
    squares, refs = refs[:count], refs[count:]
    parts, refs = refs[:part_count], refs[part_count:]
    previous = refs[0][...] if has_previous else None
    scale_ref, out_ref, weight, sums = refs[1 if has_previous else 0 :]
    scale = new_scale(read_parts(parts), previous)
    scale_ref[...] = scale
    weight[...] = scale * scale
    sums[...] = jnp.zeros(sums.shape, jnp.float32)

    def body(step, carry):
        rows = chunk_rows(plan, step)
        weights = row_columns(plan, step, weight)
        for index in range(count):
            first = plan.first_tile(index)
            for t in range(plan.tiles[index]):
                part = squares[index][rows, lane_tile(t)] * weights[index]
                folded = jnp.sum(part.reshape(plan.chunk // 8, 8, LANES), axis=0)
                sums[first + t] = sums[first + t] + folded
        return carry

    lax.fori_loop(0, plan.chunks, body, 0, unroll=plan.unroll)
    out_ref[...] = jnp.sum(sums[...], axis=1) * plan.col_inv


def scale_kernel(plan, held, row_scale, out_ref):
    def body(step, carry):
        rows = chunk_rows(plan, step)
        weights = row_columns(plan, step, row_scale)
        for index in range(plan.count):
            weight = jnp.concatenate([weights[index]] * plan.group[index], axis=1)
            for t in range(0, plan.tiles[index], plan.group[index]):
                span = plan.span(index, t)
                out_ref[rows, span] = held[rows, span].astype(jnp.float32) * weight
        return carry

    lax.fori_loop(0, plan.chunks, body, 0, unroll=min(2, plan.chunks))


def last_kernel(plan, part_count, *refs):
    count = plan.count
    scaled, refs = refs[0], refs[1:]
    parts, refs = refs[:part_count], refs[part_count:]
    previous, refs = refs[0], refs[1:]
    outs, refs = refs[:count], refs[count:]
    col_scale, stage, sems = refs
    col_scale[...] = new_scale(read_parts(parts), previous[...])

    def copy(step, index):
        rows = chunk_rows(plan, step)
        cols = pl.ds(plan.starts[index], plan.cols[index])
        return pltpu.make_async_copy(
            stage.at[rows, cols], outs[index].at[rows], sems.at[step]
        )

    def body(step, carry):
        rows = chunk_rows(plan, step)
        for index in range(count):
            first = plan.first_tile(index)
            group = plan.group[index]
            for t in range(0, plan.tiles[index], group):
                span = plan.span(index, t)
                cols = [col_scale[first + t + k : first + t + k + 1, :] for k in range(group)]
                value = scaled[rows, span] * jnp.concatenate(cols, axis=1)
                stage[rows, span] = value.astype(stage.dtype)
        for index in range(count):
            copy(step, index).start()
        return carry

    lax.fori_loop(0, plan.chunks, body, 0, unroll=2)
    for step in range(plan.chunks):
        sent = stage.at[chunk_rows(plan, step)]
        pltpu.make_async_copy(sent, sent, sems.at[step]).wait()


def exchange_rows(part):
    size = lax.axis_size("mp")
    if size > DIRECT_LIMIT or size & (size - 1):
        return [lax.psum(part, "mp")]
    parts = [part]
    for offset in range(1, size):
        pairs = [(index, index ^ offset) for index in range(size)]
        parts.append(lax.ppermute(part, "mp", pairs))
    return parts


def exchange_cols(part):
    size = lax.axis_size("dp")
    if size > DIRECT_LIMIT or size & (size - 1):
        return [lax.psum(part, "dp")]
    if size == 1:
        return [part]
    pair = part + lax.ppermute(part, "dp", [(index, index ^ 1) for index in range(size)])
    parts = [pair]
    for offset in range(2, size, 2):
        parts.append(lax.ppermute(pair, "dp", [(index, index ^ offset) for index in range(size)]))
    return parts


def shards(q_grad, k_grad, v_grad, o_grad):
    grads = (q_grad, k_grad, v_grad, o_grad)
    plan = Plan(grads)
    count = plan.count
    f32 = jnp.float32
    row_out = VM(plan.row_shape, f32)
    col_out = VM(plan.col_shape, f32)

    loaded = pl.pallas_call(
        functools.partial(load_kernel, plan),
        in_specs=[OUTSIDE] * count,
        out_specs=[WHOLE] * (count + 2),
        out_shape=[VM(plan.wide, grads[0].dtype)]
        + [VM(grad.shape, f32) for grad in grads]
        + [row_out],
        scratch_shapes=[pltpu.SemaphoreType.DMA((plan.chunks,))],
        compiler_params=PARAMS,
        name="load",
    )(*[pltpu.with_memory_space_constraint(grad, pltpu.HBM) for grad in grads])
    held, squares, row_part = loaded[0], loaded[1 : 1 + count], loaded[1 + count]

    row_scale = col_scale = None
    for sweep in range(ITERS):
        parts = exchange_rows(row_part)
        previous = [] if row_scale is None else [row_scale]
        row_scale, col_part = pl.pallas_call(
            functools.partial(col_kernel, plan, len(parts), bool(previous)),
            in_specs=[WHOLE] * (count + len(parts) + len(previous)),
            out_specs=[WHOLE] * 2,
            out_shape=[row_out, col_out],
            scratch_shapes=[
                VM(plan.row_shape, f32),
                VM((plan.col_shape[0], 8, LANES), f32),
            ],
            compiler_params=PARAMS,
            name=f"col{sweep}",
        )(*squares, *parts, *previous)
        parts = exchange_cols(col_part)
        previous = [] if col_scale is None else [col_scale]
        if sweep + 1 == ITERS:
            break
        col_scale, row_part = pl.pallas_call(
            functools.partial(row_kernel, plan, len(parts), bool(previous)),
            in_specs=[WHOLE] * (count + len(parts) + len(previous)),
            out_specs=[WHOLE] * 2,
            out_shape=[col_out, row_out],
            scratch_shapes=[VM(plan.col_shape, f32)],
            compiler_params=PARAMS,
            name=f"row{sweep}",
        )(*squares, *parts, *previous)

    size = plan.wide[0] * plan.wide[1]
    scaled = pl.pallas_call(
        functools.partial(scale_kernel, plan),
        in_specs=[WHOLE] * 2,
        out_specs=WHOLE,
        out_shape=VM(plan.wide, f32),
        compiler_params=PARAMS,
        cost_estimate=pl.CostEstimate(flops=2 * size, bytes_accessed=6 * size, transcendentals=0),
        name="scale",
    )(held, row_scale)
    return tuple(
        pl.pallas_call(
            functools.partial(last_kernel, plan, len(parts)),
            in_specs=[WHOLE] * (len(parts) + 2),
            out_specs=[OUTSIDE] * count,
            out_shape=[jax.ShapeDtypeStruct(grad.shape, grad.dtype) for grad in grads],
            scratch_shapes=[VM(plan.col_shape, f32)]
            + [VM(plan.wide, grads[0].dtype)]
            + [pltpu.SemaphoreType.DMA((plan.chunks,))],
            compiler_params=PARAMS,
            name="last",
        )(scaled, *parts, col_scale)
    )


def solution(mesh):
    return jax.shard_map(
        shards,
        mesh=mesh,
        in_specs=(P("dp", "mp"), P("dp", "mp"), P("dp", "mp"), P("dp", "mp")),
        out_specs=(P("dp", "mp"), P("dp", "mp"), P("dp", "mp"), P("dp", "mp")),
        check_vma=False,
    )
```

```python
import functools

import jax
import jax.numpy as jnp
from jax import lax
from jax.experimental import pallas as pl
from jax.experimental.pallas import tpu as pltpu
from jax.sharding import PartitionSpec as P

ITERS = 3
EPSILON = 1e-06
LANES = 128
DIRECT_LIMIT = 8
UNROLL = 8
ROW_UNROLL = 4

VM = pltpu.VMEM
WHOLE = pl.BlockSpec(memory_space=pltpu.VMEM)
OUTSIDE = pl.BlockSpec(memory_space=pltpu.HBM)
PARAMS = pltpu.CompilerParams(vmem_limit_bytes=16 << 20)


class Plan:
    def __init__(self, grads):
        self.count = len(grads)
        self.rows = grads[0].shape[0]
        self.cols = [grad.shape[1] for grad in grads]
        self.chunk = min(LANES, self.rows)
        self.chunks = self.rows // self.chunk
        self.unroll = min(UNROLL, self.chunks)
        self.tiles = [n // LANES for n in self.cols]
        self.group = [2 if t % 2 == 0 else 1 for t in self.tiles]
        self.starts = [sum(self.cols[:index]) for index in range(self.count)]
        self.wide = (self.rows, sum(self.cols))
        self.row_inv = [1.0 / float(n * lax.axis_size("mp")) for n in self.cols]
        self.col_inv = 1.0 / float(self.rows * lax.axis_size("dp"))
        self.row_shape = (self.chunks * self.count, LANES)
        self.col_shape = (-(-sum(self.tiles) // 8) * 8, LANES)

    def span(self, index, t):
        return pl.ds(self.starts[index] + t * LANES, self.group[index] * LANES)

    def first_tile(self, index):
        return sum(self.tiles[:index])


def lane_tile(t):
    return pl.ds(t * LANES, LANES)


def chunk_rows(plan, step):
    return pl.ds(pl.multiple_of(step * plan.chunk, plan.chunk), plan.chunk)


def put_row_sums(plan, step, sums, out_ref):
    lane = lax.broadcasted_iota(jnp.int32, sums[0].shape[:1] + (LANES,), 1)
    merged = jnp.broadcast_to(sums[0], lane.shape)
    for index in range(1, plan.count):
        merged = jnp.where(lane == index, sums[index], merged)
    put_merged(plan, step, merged, out_ref)


def put_merged(plan, step, merged, out_ref):
    turned = merged.T[0 : plan.count, :]
    place = lax.broadcasted_iota(jnp.int32, turned.shape, 0)
    scale = jnp.full(turned.shape, plan.row_inv[0], jnp.float32)
    for index in range(1, plan.count):
        scale = jnp.where(place == index, plan.row_inv[index], scale)
    out_ref[pl.ds(step * plan.count, plan.count), 0 : plan.chunk] = turned * scale


def turned_columns(plan, step, ref):
    block = ref[pl.ds(step * plan.count, plan.count), 0 : plan.chunk]
    block = jnp.concatenate([block, jnp.zeros((8 - plan.count, plan.chunk), jnp.float32)], axis=0)
    return block.T


def row_columns(plan, step, ref):
    turned = turned_columns(plan, step, ref)
    return [
        jnp.broadcast_to(turned[:, index : index + 1], (plan.chunk, LANES))
        for index in range(plan.count)
    ]


def new_scale(parts, previous):
    total = parts[0]
    for part in parts[1:]:
        total = total + part
    if previous is None:
        return lax.rsqrt(total + EPSILON)
    return previous * lax.rsqrt(previous * previous * total + EPSILON)


def load_kernel(plan, *refs):
    count = plan.count
    sources, held, squares = refs[:count], refs[count], refs[count + 1 : 2 * count + 1]
    out_ref, sems = refs[2 * count + 1 :]

    def copy(step, index):
        rows = chunk_rows(plan, step)
        cols = pl.ds(plan.starts[index], plan.cols[index])
        return pltpu.make_async_copy(
            sources[index].at[rows], held.at[rows, cols], sems.at[step]
        )

    out_ref[...] = jnp.zeros(plan.row_shape, jnp.float32)
    for step in range(plan.chunks):
        for index in range(count):
            copy(step, index).start()

    def body(step, carry):
        rows = chunk_rows(plan, step)
        sums = []
        arrived = held.at[rows]
        pltpu.make_async_copy(arrived, arrived, sems.at[step]).wait()
        for index in range(count):
            total = None
            group = plan.group[index]
            for t in range(0, plan.tiles[index], group):
                span = pl.ds(t * LANES, group * LANES)
                wide = held[rows, plan.span(index, t)].astype(jnp.float32)
                square = wide * wide
                squares[index][rows, span] = square
                for k in range(group):
                    part = square[:, k * LANES : (k + 1) * LANES]
                    total = part if total is None else total + part
            sums.append(jnp.sum(total, axis=1, keepdims=True))
        put_row_sums(plan, step, sums, out_ref)
        return carry

    lax.fori_loop(0, plan.chunks, body, 0)


def row_kernel(plan, part_count, has_previous, *refs):
    count = plan.count
    squares, refs = refs[:count], refs[count:]
    parts, refs = refs[:part_count], refs[part_count:]
    previous = refs[0][...] if has_previous else None
    scale_ref, out_ref, weight = refs[1 if has_previous else 0 :]
    scale = new_scale(read_parts(parts), previous)
    scale_ref[...] = scale
    weight[...] = scale * scale
    out_ref[...] = jnp.zeros(plan.row_shape, jnp.float32)

    weights = [jnp.broadcast_to(weight[t : t + 1, :], (8, LANES)) for t in range(sum(plan.tiles))]

    def body(step, carry):
        lane = lax.broadcasted_iota(jnp.int32, (8, LANES), 1)
        merged = []
        for group in range(plan.chunk // 8):
            rows = pl.ds(pl.multiple_of(step * plan.chunk + group * 8, 8), 8)
            line = None
            for index in range(count):
                first = plan.first_tile(index)
                total = None
                for t in range(plan.tiles[index]):
                    part = squares[index][rows, lane_tile(t)] * weights[first + t]
                    total = part if total is None else total + part
                total = jnp.broadcast_to(jnp.sum(total, axis=1, keepdims=True), (8, LANES))
                line = total if line is None else jnp.where(lane == index, total, line)
            merged.append(line)
        put_merged(plan, step, jnp.concatenate(merged, axis=0), out_ref)
        return carry

    lax.fori_loop(0, plan.chunks, body, 0, unroll=min(ROW_UNROLL, plan.chunks))


def read_parts(parts):
    values = []
    for part in parts:
        if len(part.shape) == 3:
            values.extend(part[slot] for slot in range(part.shape[0]))
        else:
            values.append(part[...])
    return values


def col_kernel(plan, part_count, has_previous, *refs):
    count = plan.count
    squares, refs = refs[:count], refs[count:]
    parts, refs = refs[:part_count], refs[part_count:]
    previous = refs[0][...] if has_previous else None
    scale_ref, out_ref, weight, sums = refs[1 if has_previous else 0 :]
    scale = new_scale(read_parts(parts), previous)
    scale_ref[...] = scale
    weight[...] = scale * scale
    sums[...] = jnp.zeros(sums.shape, jnp.float32)

    def body(step, carry):
        turned = turned_columns(plan, step, weight)
        size = min(64, plan.chunk)
        for start in range(0, plan.chunk, size):
            rows = pl.ds(pl.multiple_of(step * plan.chunk + start, size), size)
            for index in range(count):
                first = plan.first_tile(index)
                column = turned[start : start + size, index : index + 1]
                spread = jnp.broadcast_to(column, (size, LANES))
                for t in range(plan.tiles[index]):
                    part = squares[index][rows, lane_tile(t)] * spread
                    folded = jnp.sum(part.reshape(size // 8, 8, LANES), axis=0)
                    sums[first + t] = sums[first + t] + folded
        return carry

    lax.fori_loop(0, plan.chunks, body, 0, unroll=plan.unroll)
    out_ref[...] = jnp.sum(sums[...], axis=1) * plan.col_inv


def scale_kernel(plan, held, row_scale, out_ref):
    def body(step, carry):
        rows = chunk_rows(plan, step)
        weights = row_columns(plan, step, row_scale)
        for index in range(plan.count):
            weight = jnp.concatenate([weights[index]] * plan.group[index], axis=1)
            for t in range(0, plan.tiles[index], plan.group[index]):
                span = plan.span(index, t)
                out_ref[rows, span] = held[rows, span].astype(jnp.float32) * weight
        return carry

    lax.fori_loop(0, plan.chunks, body, 0, unroll=min(2, plan.chunks))


def last_kernel(plan, part_count, *refs):
    count = plan.count
    scaled, refs = refs[0], refs[1:]
    parts, refs = refs[:part_count], refs[part_count:]
    previous, refs = refs[0], refs[1:]
    outs, refs = refs[:count], refs[count:]
    col_scale, stage, sems = refs
    col_scale[...] = new_scale(read_parts(parts), previous[...])

    def copy(step, index):
        rows = chunk_rows(plan, step)
        cols = pl.ds(plan.starts[index], plan.cols[index])
        return pltpu.make_async_copy(
            stage.at[rows, cols], outs[index].at[rows], sems.at[step]
        )

    def body(step, carry):
        rows = chunk_rows(plan, step)
        for index in range(count):
            first = plan.first_tile(index)
            group = plan.group[index]
            for t in range(0, plan.tiles[index], group):
                span = plan.span(index, t)
                cols = [col_scale[first + t + k : first + t + k + 1, :] for k in range(group)]
                value = scaled[rows, span] * jnp.concatenate(cols, axis=1)
                stage[rows, span] = value.astype(stage.dtype)
        for index in range(count):
            copy(step, index).start()
        return carry

    lax.fori_loop(0, plan.chunks, body, 0, unroll=2)
    for step in range(plan.chunks):
        sent = stage.at[chunk_rows(plan, step)]
        pltpu.make_async_copy(sent, sent, sems.at[step]).wait()


def exchange_rows(part):
    size = lax.axis_size("mp")
    if size > DIRECT_LIMIT or size & (size - 1):
        return [lax.psum(part, "mp")]
    parts = [part]
    for offset in range(1, size):
        pairs = [(index, index ^ offset) for index in range(size)]
        parts.append(lax.ppermute(part, "mp", pairs))
    return parts


def exchange_cols(part):
    size = lax.axis_size("dp")
    if size > DIRECT_LIMIT or size & (size - 1):
        return [lax.psum(part, "dp")]
    if size == 1:
        return [part]
    pair = part + lax.ppermute(part, "dp", [(index, index ^ 1) for index in range(size)])
    parts = [pair]
    for offset in range(2, size, 2):
        parts.append(lax.ppermute(pair, "dp", [(index, index ^ offset) for index in range(size)]))
    return parts


def shards(q_grad, k_grad, v_grad, o_grad):
    grads = (q_grad, k_grad, v_grad, o_grad)
    plan = Plan(grads)
    count = plan.count
    f32 = jnp.float32
    row_out = VM(plan.row_shape, f32)
    col_out = VM(plan.col_shape, f32)

    loaded = pl.pallas_call(
        functools.partial(load_kernel, plan),
        in_specs=[OUTSIDE] * count,
        out_specs=[WHOLE] * (count + 2),
        out_shape=[VM(plan.wide, grads[0].dtype)]
        + [VM(grad.shape, f32) for grad in grads]
        + [row_out],
        scratch_shapes=[pltpu.SemaphoreType.DMA((plan.chunks,))],
        compiler_params=PARAMS,
        name="load",
    )(*[pltpu.with_memory_space_constraint(grad, pltpu.HBM) for grad in grads])
    held, squares, row_part = loaded[0], loaded[1 : 1 + count], loaded[1 + count]

    row_scale = col_scale = None
    for sweep in range(ITERS):
        parts = exchange_rows(row_part)
        previous = [] if row_scale is None else [row_scale]
        row_scale, col_part = pl.pallas_call(
            functools.partial(col_kernel, plan, len(parts), bool(previous)),
            in_specs=[WHOLE] * (count + len(parts) + len(previous)),
            out_specs=[WHOLE] * 2,
            out_shape=[row_out, col_out],
            scratch_shapes=[
                VM(plan.row_shape, f32),
                VM((plan.col_shape[0], 8, LANES), f32),
            ],
            compiler_params=PARAMS,
            name=f"col{sweep}",
        )(*squares, *parts, *previous)
        parts = exchange_cols(col_part)
        previous = [] if col_scale is None else [col_scale]
        if sweep + 1 == ITERS:
            break
        col_scale, row_part = pl.pallas_call(
            functools.partial(row_kernel, plan, len(parts), bool(previous)),
            in_specs=[WHOLE] * (count + len(parts) + len(previous)),
            out_specs=[WHOLE] * 2,
            out_shape=[col_out, row_out],
            scratch_shapes=[VM(plan.col_shape, f32)],
            compiler_params=PARAMS,
            name=f"row{sweep}",
        )(*squares, *parts, *previous)

    size = plan.wide[0] * plan.wide[1]
    scaled = pl.pallas_call(
        functools.partial(scale_kernel, plan),
        in_specs=[WHOLE] * 2,
        out_specs=WHOLE,
        out_shape=VM(plan.wide, f32),
        compiler_params=PARAMS,
        cost_estimate=pl.CostEstimate(flops=2 * size, bytes_accessed=6 * size, transcendentals=0),
        name="scale",
    )(held, row_scale)
    return tuple(
        pl.pallas_call(
            functools.partial(last_kernel, plan, len(parts)),
            in_specs=[WHOLE] * (len(parts) + 2),
            out_specs=[OUTSIDE] * count,
            out_shape=[jax.ShapeDtypeStruct(grad.shape, grad.dtype) for grad in grads],
            scratch_shapes=[VM(plan.col_shape, f32)]
            + [VM(plan.wide, grads[0].dtype)]
            + [pltpu.SemaphoreType.DMA((plan.chunks,))],
            compiler_params=PARAMS,
            name="last",
        )(scaled, *parts, col_scale)
    )


def solution(mesh):
    return jax.shard_map(
        shards,
        mesh=mesh,
        in_specs=(P("dp", "mp"), P("dp", "mp"), P("dp", "mp"), P("dp", "mp")),
        out_specs=(P("dp", "mp"), P("dp", "mp"), P("dp", "mp"), P("dp", "mp")),
        check_vma=False,
    )
```

```python
import functools

import jax
import jax.numpy as jnp
from jax import lax
from jax.experimental import pallas as pl
from jax.experimental.pallas import tpu as pltpu
from jax.sharding import PartitionSpec as P

ITERS = 3
EPSILON = 1e-06
LANES = 128
DIRECT_LIMIT = 8
UNROLL = 8
ROW_UNROLL = 4

VM = pltpu.VMEM
WHOLE = pl.BlockSpec(memory_space=pltpu.VMEM)
OUTSIDE = pl.BlockSpec(memory_space=pltpu.HBM)
PARAMS = pltpu.CompilerParams(vmem_limit_bytes=16 << 20)


class Plan:
    def __init__(self, grads):
        self.count = len(grads)
        self.rows = grads[0].shape[0]
        self.cols = [grad.shape[1] for grad in grads]
        self.chunk = min(LANES, self.rows)
        self.chunks = self.rows // self.chunk
        self.unroll = min(UNROLL, self.chunks)
        self.tiles = [n // LANES for n in self.cols]
        self.group = [2 if t % 2 == 0 else 1 for t in self.tiles]
        self.starts = [sum(self.cols[:index]) for index in range(self.count)]
        self.wide = (self.rows, sum(self.cols))
        self.row_inv = [1.0 / float(n * lax.axis_size("mp")) for n in self.cols]
        self.col_inv = 1.0 / float(self.rows * lax.axis_size("dp"))
        self.row_shape = (self.chunks * self.count, LANES)
        self.col_shape = (-(-sum(self.tiles) // 8) * 8, LANES)

    def span(self, index, t):
        return pl.ds(self.starts[index] + t * LANES, self.group[index] * LANES)

    def first_tile(self, index):
        return sum(self.tiles[:index])


def lane_tile(t):
    return pl.ds(t * LANES, LANES)


def chunk_rows(plan, step):
    return pl.ds(pl.multiple_of(step * plan.chunk, plan.chunk), plan.chunk)


def put_row_sums(plan, step, sums, out_ref):
    lane = lax.broadcasted_iota(jnp.int32, sums[0].shape[:1] + (LANES,), 1)
    merged = jnp.broadcast_to(sums[0], lane.shape)
    for index in range(1, plan.count):
        merged = jnp.where(lane == index, sums[index], merged)
    put_merged(plan, step, merged, out_ref)


def put_merged(plan, step, merged, out_ref):
    turned = merged.T[0 : plan.count, :]
    place = lax.broadcasted_iota(jnp.int32, turned.shape, 0)
    scale = jnp.full(turned.shape, plan.row_inv[0], jnp.float32)
    for index in range(1, plan.count):
        scale = jnp.where(place == index, plan.row_inv[index], scale)
    out_ref[pl.ds(step * plan.count, plan.count), 0 : plan.chunk] = turned * scale


def turned_columns(plan, step, ref):
    block = ref[pl.ds(step * plan.count, plan.count), 0 : plan.chunk]
    block = jnp.concatenate([block, jnp.zeros((8 - plan.count, plan.chunk), jnp.float32)], axis=0)
    return block.T


def new_scale(parts, previous):
    total = parts[0]
    for part in parts[1:]:
        total = total + part
    if previous is None:
        return lax.rsqrt(total + EPSILON)
    return previous * lax.rsqrt(previous * previous * total + EPSILON)


def load_kernel(plan, *refs):
    count = plan.count
    sources, held, squares = refs[:count], refs[count], refs[count + 1 : 2 * count + 1]
    out_ref, sems = refs[2 * count + 1 :]

    def copy(step, index):
        rows = chunk_rows(plan, step)
        cols = pl.ds(plan.starts[index], plan.cols[index])
        return pltpu.make_async_copy(
            sources[index].at[rows], held.at[rows, cols], sems.at[step]
        )

    out_ref[...] = jnp.zeros(plan.row_shape, jnp.float32)
    for step in range(plan.chunks):
        for index in range(count):
            copy(step, index).start()

    def body(step, carry):
        rows = chunk_rows(plan, step)
        sums = []
        arrived = held.at[rows]
        pltpu.make_async_copy(arrived, arrived, sems.at[step]).wait()
        for index in range(count):
            total = None
            group = plan.group[index]
            for t in range(0, plan.tiles[index], group):
                span = pl.ds(t * LANES, group * LANES)
                wide = held[rows, plan.span(index, t)].astype(jnp.float32)
                square = wide * wide
                squares[index][rows, span] = square
                for k in range(group):
                    part = square[:, k * LANES : (k + 1) * LANES]
                    total = part if total is None else total + part
            sums.append(jnp.sum(total, axis=1, keepdims=True))
        put_row_sums(plan, step, sums, out_ref)
        return carry

    lax.fori_loop(0, plan.chunks, body, 0)


def row_kernel(plan, part_count, has_previous, *refs):
    count = plan.count
    squares, refs = refs[:count], refs[count:]
    parts, refs = refs[:part_count], refs[part_count:]
    previous = refs[0][...] if has_previous else None
    scale_ref, out_ref, weight = refs[1 if has_previous else 0 :]
    scale = new_scale(read_parts(parts), previous)
    scale_ref[...] = scale
    weight[...] = scale * scale
    out_ref[...] = jnp.zeros(plan.row_shape, jnp.float32)

    weights = [jnp.broadcast_to(weight[t : t + 1, :], (8, LANES)) for t in range(sum(plan.tiles))]

    def body(step, carry):
        lane = lax.broadcasted_iota(jnp.int32, (8, LANES), 1)
        merged = []
        for group in range(plan.chunk // 8):
            rows = pl.ds(pl.multiple_of(step * plan.chunk + group * 8, 8), 8)
            line = None
            for index in range(count):
                first = plan.first_tile(index)
                total = None
                for t in range(plan.tiles[index]):
                    part = squares[index][rows, lane_tile(t)] * weights[first + t]
                    total = part if total is None else total + part
                total = jnp.broadcast_to(jnp.sum(total, axis=1, keepdims=True), (8, LANES))
                line = total if line is None else jnp.where(lane == index, total, line)
            merged.append(line)
        put_merged(plan, step, jnp.concatenate(merged, axis=0), out_ref)
        return carry

    lax.fori_loop(0, plan.chunks, body, 0, unroll=min(ROW_UNROLL, plan.chunks))


def read_parts(parts):
    values = []
    for part in parts:
        if len(part.shape) == 3:
            values.extend(part[slot] for slot in range(part.shape[0]))
        else:
            values.append(part[...])
    return values


def col_kernel(plan, part_count, has_previous, *refs):
    count = plan.count
    squares, refs = refs[:count], refs[count:]
    parts, refs = refs[:part_count], refs[part_count:]
    previous = refs[0][...] if has_previous else None
    scale_ref, out_ref, weight, sums = refs[1 if has_previous else 0 :]
    scale = new_scale(read_parts(parts), previous)
    scale_ref[...] = scale
    weight[...] = scale * scale
    sums[...] = jnp.zeros(sums.shape, jnp.float32)

    def body(step, carry):
        turned = turned_columns(plan, step, weight)
        size = min(64, plan.chunk)
        for start in range(0, plan.chunk, size):
            rows = pl.ds(pl.multiple_of(step * plan.chunk + start, size), size)
            for index in range(count):
                first = plan.first_tile(index)
                column = turned[start : start + size, index : index + 1]
                spread = jnp.broadcast_to(column, (size, LANES))
                for t in range(plan.tiles[index]):
                    part = squares[index][rows, lane_tile(t)] * spread
                    folded = jnp.sum(part.reshape(size // 8, 8, LANES), axis=0)
                    sums[first + t] = sums[first + t] + folded
        return carry

    lax.fori_loop(0, plan.chunks, body, 0, unroll=plan.unroll)
    out_ref[...] = jnp.sum(sums[...], axis=1) * plan.col_inv


def scale_kernel(plan, held, row_scale, out_ref):
    def body(step, carry):
        turned = turned_columns(plan, step, row_scale)
        size = min(64, plan.chunk)
        for start in range(0, plan.chunk, size):
            rows = pl.ds(pl.multiple_of(step * plan.chunk + start, size), size)
            for index in range(plan.count):
                group = plan.group[index]
                column = turned[start : start + size, index : index + 1]
                weight = jnp.broadcast_to(column, (size, group * LANES))
                for t in range(0, plan.tiles[index], group):
                    span = plan.span(index, t)
                    out_ref[rows, span] = held[rows, span].astype(jnp.float32) * weight
        return carry

    lax.fori_loop(0, plan.chunks, body, 0, unroll=min(8, plan.chunks))


def last_kernel(plan, part_count, *refs):
    count = plan.count
    scaled, refs = refs[0], refs[1:]
    parts, refs = refs[:part_count], refs[part_count:]
    previous, refs = refs[0], refs[1:]
    outs, refs = refs[:count], refs[count:]
    col_scale, stage, sems = refs
    col_scale[...] = new_scale(read_parts(parts), previous[...])

    def copy(step, index):
        rows = chunk_rows(plan, step)
        cols = pl.ds(plan.starts[index], plan.cols[index])
        return pltpu.make_async_copy(
            stage.at[rows, cols], outs[index].at[rows], sems.at[step]
        )

    def body(step, carry):
        rows = chunk_rows(plan, step)
        for index in range(count):
            first = plan.first_tile(index)
            group = plan.group[index]
            for t in range(0, plan.tiles[index], group):
                span = plan.span(index, t)
                cols = [col_scale[first + t + k : first + t + k + 1, :] for k in range(group)]
                value = scaled[rows, span] * jnp.concatenate(cols, axis=1)
                stage[rows, span] = value.astype(stage.dtype)
        for index in range(count):
            copy(step, index).start()
        return carry

    lax.fori_loop(0, plan.chunks, body, 0, unroll=2)
    for step in range(plan.chunks):
        sent = stage.at[chunk_rows(plan, step)]
        pltpu.make_async_copy(sent, sent, sems.at[step]).wait()


def exchange_rows(part):
    size = lax.axis_size("mp")
    if size > DIRECT_LIMIT or size & (size - 1):
        return [lax.psum(part, "mp")]
    parts = [part]
    for offset in range(1, size):
        pairs = [(index, index ^ offset) for index in range(size)]
        parts.append(lax.ppermute(part, "mp", pairs))
    return parts


def exchange_cols(part, beside=None):
    size = lax.axis_size("dp")
    if size > DIRECT_LIMIT or size & (size - 1):
        return [lax.psum(part, "dp")]
    if size == 1:
        return [part]
    pair = part + lax.ppermute(part, "dp", [(index, index ^ 1) for index in range(size)])
    if beside is not None:
        pair = lax.optimization_barrier((pair, beside))[0]
    parts = [pair]
    for offset in range(2, size, 2):
        parts.append(lax.ppermute(pair, "dp", [(index, index ^ offset) for index in range(size)]))
    return parts


def scale_rows(plan, held, row_scale):
    size = plan.wide[0] * plan.wide[1]
    return pl.pallas_call(
        functools.partial(scale_kernel, plan),
        in_specs=[WHOLE] * 2,
        out_specs=WHOLE,
        out_shape=VM(plan.wide, jnp.float32),
        compiler_params=PARAMS,
        cost_estimate=pl.CostEstimate(flops=2 * size, bytes_accessed=6 * size, transcendentals=0),
        name="scale",
    )(held, row_scale)


def shards(q_grad, k_grad, v_grad, o_grad):
    grads = (q_grad, k_grad, v_grad, o_grad)
    plan = Plan(grads)
    count = plan.count
    f32 = jnp.float32
    row_out = VM(plan.row_shape, f32)
    col_out = VM(plan.col_shape, f32)

    loaded = pl.pallas_call(
        functools.partial(load_kernel, plan),
        in_specs=[OUTSIDE] * count,
        out_specs=[WHOLE] * (count + 2),
        out_shape=[VM(plan.wide, grads[0].dtype)]
        + [VM(grad.shape, f32) for grad in grads]
        + [row_out],
        scratch_shapes=[pltpu.SemaphoreType.DMA((plan.chunks,))],
        compiler_params=PARAMS,
        name="load",
    )(*[pltpu.with_memory_space_constraint(grad, pltpu.HBM) for grad in grads])
    held, squares, row_part = loaded[0], loaded[1 : 1 + count], loaded[1 + count]

    row_scale = col_scale = None
    for sweep in range(ITERS):
        parts = exchange_rows(row_part)
        previous = [] if row_scale is None else [row_scale]
        row_scale, col_part = pl.pallas_call(
            functools.partial(col_kernel, plan, len(parts), bool(previous)),
            in_specs=[WHOLE] * (count + len(parts) + len(previous)),
            out_specs=[WHOLE] * 2,
            out_shape=[row_out, col_out],
            scratch_shapes=[
                VM(plan.row_shape, f32),
                VM((plan.col_shape[0], 8, LANES), f32),
            ],
            compiler_params=PARAMS,
            name=f"col{sweep}",
        )(*squares, *parts, *previous)
        scaled = scale_rows(plan, held, row_scale) if sweep + 1 == ITERS else None
        parts = exchange_cols(col_part, scaled)
        previous = [] if col_scale is None else [col_scale]
        if sweep + 1 == ITERS:
            break
        col_scale, row_part = pl.pallas_call(
            functools.partial(row_kernel, plan, len(parts), bool(previous)),
            in_specs=[WHOLE] * (count + len(parts) + len(previous)),
            out_specs=[WHOLE] * 2,
            out_shape=[col_out, row_out],
            scratch_shapes=[VM(plan.col_shape, f32)],
            compiler_params=PARAMS,
            name=f"row{sweep}",
        )(*squares, *parts, *previous)

    return tuple(
        pl.pallas_call(
            functools.partial(last_kernel, plan, len(parts)),
            in_specs=[WHOLE] * (len(parts) + 2),
            out_specs=[OUTSIDE] * count,
            out_shape=[jax.ShapeDtypeStruct(grad.shape, grad.dtype) for grad in grads],
            scratch_shapes=[VM(plan.col_shape, f32)]
            + [VM(plan.wide, grads[0].dtype)]
            + [pltpu.SemaphoreType.DMA((plan.chunks,))],
            compiler_params=PARAMS,
            name="last",
        )(scaled, *parts, col_scale)
    )


def solution(mesh):
    return jax.shard_map(
        shards,
        mesh=mesh,
        in_specs=(P("dp", "mp"), P("dp", "mp"), P("dp", "mp"), P("dp", "mp")),
        out_specs=(P("dp", "mp"), P("dp", "mp"), P("dp", "mp"), P("dp", "mp")),
        check_vma=False,
    )
```

```python
import functools

import jax
import jax.numpy as jnp
from jax import lax
from jax.experimental import pallas as pl
from jax.experimental.pallas import tpu as pltpu
from jax.sharding import PartitionSpec as P

ITERS = 3
EPSILON = 1e-06
LANES = 128
DIRECT_LIMIT = 8
UNROLL = 8
ROW_UNROLL = 4

VM = pltpu.VMEM
WHOLE = pl.BlockSpec(memory_space=pltpu.VMEM)
OUTSIDE = pl.BlockSpec(memory_space=pltpu.HBM)
PARAMS = pltpu.CompilerParams(vmem_limit_bytes=16 << 20)


class Plan:
    def __init__(self, grads):
        self.count = len(grads)
        self.rows = grads[0].shape[0]
        self.cols = [grad.shape[1] for grad in grads]
        self.chunk = min(LANES, self.rows)
        self.chunks = self.rows // self.chunk
        self.unroll = min(UNROLL, self.chunks)
        self.tiles = [n // LANES for n in self.cols]
        self.group = [2 if t % 2 == 0 else 1 for t in self.tiles]
        self.starts = [sum(self.cols[:index]) for index in range(self.count)]
        self.wide = (self.rows, sum(self.cols))
        self.row_inv = [1.0 / float(n * lax.axis_size("mp")) for n in self.cols]
        self.col_inv = 1.0 / float(self.rows * lax.axis_size("dp"))
        self.row_shape = (self.chunks * self.count, LANES)
        self.col_shape = (-(-sum(self.tiles) // 8) * 8, LANES)

    def span(self, index, t):
        return pl.ds(self.starts[index] + t * LANES, self.group[index] * LANES)

    def first_tile(self, index):
        return sum(self.tiles[:index])


def lane_tile(t):
    return pl.ds(t * LANES, LANES)


def chunk_rows(plan, step):
    return pl.ds(pl.multiple_of(step * plan.chunk, plan.chunk), plan.chunk)


def put_row_sums(plan, step, sums, out_ref):
    lane = lax.broadcasted_iota(jnp.int32, sums[0].shape[:1] + (LANES,), 1)
    merged = jnp.broadcast_to(sums[0], lane.shape)
    for index in range(1, plan.count):
        merged = jnp.where(lane == index, sums[index], merged)
    put_merged(plan, step, merged, out_ref)


def put_merged(plan, step, merged, out_ref):
    turned = merged.T[0 : plan.count, :]
    place = lax.broadcasted_iota(jnp.int32, turned.shape, 0)
    scale = jnp.full(turned.shape, plan.row_inv[0], jnp.float32)
    for index in range(1, plan.count):
        scale = jnp.where(place == index, plan.row_inv[index], scale)
    out_ref[pl.ds(step * plan.count, plan.count), 0 : plan.chunk] = turned * scale


def turned_columns(plan, step, ref):
    block = ref[pl.ds(step * plan.count, plan.count), 0 : plan.chunk]
    block = jnp.concatenate([block, jnp.zeros((8 - plan.count, plan.chunk), jnp.float32)], axis=0)
    return block.T


def new_scale(parts, previous):
    total = parts[0]
    for part in parts[1:]:
        total = total + part
    if previous is None:
        return lax.rsqrt(total + EPSILON)
    return previous * lax.rsqrt(previous * previous * total + EPSILON)


def load_kernel(plan, *refs):
    count = plan.count
    sources, held, squares = refs[:count], refs[count], refs[count + 1 : 2 * count + 1]
    out_ref, sems = refs[2 * count + 1 :]

    def copy(step, index):
        rows = chunk_rows(plan, step)
        cols = pl.ds(plan.starts[index], plan.cols[index])
        return pltpu.make_async_copy(
            sources[index].at[rows], held.at[rows, cols], sems.at[step]
        )

    out_ref[...] = jnp.zeros(plan.row_shape, jnp.float32)
    for step in range(plan.chunks):
        for index in range(count):
            copy(step, index).start()

    def body(step, carry):
        rows = chunk_rows(plan, step)
        sums = []
        arrived = held.at[rows]
        pltpu.make_async_copy(arrived, arrived, sems.at[step]).wait()
        for index in range(count):
            total = None
            group = plan.group[index]
            for t in range(0, plan.tiles[index], group):
                span = pl.ds(t * LANES, group * LANES)
                wide = held[rows, plan.span(index, t)].astype(jnp.float32)
                square = wide * wide
                squares[index][rows, span] = square
                for k in range(group):
                    part = square[:, k * LANES : (k + 1) * LANES]
                    total = part if total is None else total + part
            sums.append(jnp.sum(total, axis=1, keepdims=True))
        put_row_sums(plan, step, sums, out_ref)
        return carry

    lax.fori_loop(0, plan.chunks, body, 0)


def row_kernel(plan, part_count, has_previous, *refs):
    count = plan.count
    squares, refs = refs[:count], refs[count:]
    parts, refs = refs[:part_count], refs[part_count:]
    previous = refs[0][...] if has_previous else None
    scale_ref, out_ref, weight = refs[1 if has_previous else 0 :]
    scale = new_scale(read_parts(parts), previous)
    scale_ref[...] = scale
    weight[...] = scale * scale
    out_ref[...] = jnp.zeros(plan.row_shape, jnp.float32)

    weights = [jnp.broadcast_to(weight[t : t + 1, :], (8, LANES)) for t in range(sum(plan.tiles))]

    def body(step, carry):
        lane = lax.broadcasted_iota(jnp.int32, (8, LANES), 1)
        merged = []
        for group in range(plan.chunk // 8):
            rows = pl.ds(pl.multiple_of(step * plan.chunk + group * 8, 8), 8)
            line = None
            for index in range(count):
                first = plan.first_tile(index)
                total = None
                for t in range(plan.tiles[index]):
                    part = squares[index][rows, lane_tile(t)] * weights[first + t]
                    total = part if total is None else total + part
                total = jnp.broadcast_to(jnp.sum(total, axis=1, keepdims=True), (8, LANES))
                line = total if line is None else jnp.where(lane == index, total, line)
            merged.append(line)
        put_merged(plan, step, jnp.concatenate(merged, axis=0), out_ref)
        return carry

    lax.fori_loop(0, plan.chunks, body, 0, unroll=min(ROW_UNROLL, plan.chunks))


def read_parts(parts):
    values = []
    for part in parts:
        if len(part.shape) == 3:
            values.extend(part[slot] for slot in range(part.shape[0]))
        else:
            values.append(part[...])
    return values


def col_kernel(plan, part_count, has_previous, *refs):
    count = plan.count
    squares, refs = refs[:count], refs[count:]
    parts, refs = refs[:part_count], refs[part_count:]
    previous = refs[0][...] if has_previous else None
    scale_ref, out_ref, weight, sums = refs[1 if has_previous else 0 :]
    scale = new_scale(read_parts(parts), previous)
    scale_ref[...] = scale
    weight[...] = scale * scale
    sums[...] = jnp.zeros(sums.shape, jnp.float32)

    def body(step, carry):
        turned = turned_columns(plan, step, weight)
        size = min(64, plan.chunk)
        for start in range(0, plan.chunk, size):
            rows = pl.ds(pl.multiple_of(step * plan.chunk + start, size), size)
            for index in range(count):
                first = plan.first_tile(index)
                column = turned[start : start + size, index : index + 1]
                spread = jnp.broadcast_to(column, (size, LANES))
                for t in range(plan.tiles[index]):
                    part = squares[index][rows, lane_tile(t)] * spread
                    folded = jnp.sum(part.reshape(size // 8, 8, LANES), axis=0)
                    sums[first + t] = sums[first + t] + folded
        return carry

    lax.fori_loop(0, plan.chunks, body, 0, unroll=plan.unroll)
    out_ref[...] = jnp.sum(sums[...], axis=1) * plan.col_inv


def scale_kernel(plan, held, row_scale, out_ref):
    def body(step, carry):
        turned = turned_columns(plan, step, row_scale)
        size = min(64, plan.chunk)
        for start in range(0, plan.chunk, size):
            rows = pl.ds(pl.multiple_of(step * plan.chunk + start, size), size)
            for index in range(plan.count):
                group = plan.group[index]
                column = turned[start : start + size, index : index + 1]
                weight = jnp.broadcast_to(column, (size, group * LANES))
                for t in range(0, plan.tiles[index], group):
                    span = plan.span(index, t)
                    out_ref[rows, span] = held[rows, span].astype(jnp.float32) * weight
        return carry

    lax.fori_loop(0, plan.chunks, body, 0, unroll=min(8, plan.chunks))


def last_kernel(plan, part_count, *refs):
    count = plan.count
    scaled, refs = refs[0], refs[1:]
    parts, refs = refs[:part_count], refs[part_count:]
    previous, refs = refs[0], refs[1:]
    outs, refs = refs[:count], refs[count:]
    col_scale, stage, sems = refs
    col_scale[...] = new_scale(read_parts(parts), previous[...])

    def copy(step, index):
        rows = chunk_rows(plan, step)
        cols = pl.ds(plan.starts[index], plan.cols[index])
        return pltpu.make_async_copy(
            stage.at[rows, cols], outs[index].at[rows], sems.at[step]
        )

    def body(step, carry):
        rows = chunk_rows(plan, step)
        for index in range(count):
            first = plan.first_tile(index)
            group = plan.group[index]
            for t in range(0, plan.tiles[index], group):
                span = plan.span(index, t)
                cols = [col_scale[first + t + k : first + t + k + 1, :] for k in range(group)]
                value = scaled[rows, span] * jnp.concatenate(cols, axis=1)
                stage[rows, span] = value.astype(stage.dtype)
        for index in range(count):
            copy(step, index).start()
        return carry

    lax.fori_loop(0, plan.chunks, body, 0, unroll=2)
    for step in range(plan.chunks):
        sent = stage.at[chunk_rows(plan, step)]
        pltpu.make_async_copy(sent, sent, sems.at[step]).wait()


def exchange_rows(part):
    size = lax.axis_size("mp")
    if size > DIRECT_LIMIT or size & (size - 1):
        return [lax.psum(part, "mp")]
    parts = [part]
    for offset in range(1, size):
        pairs = [(index, index ^ offset) for index in range(size)]
        parts.append(lax.ppermute(part, "mp", pairs))
    return parts


def exchange_cols(part, beside=None):
    size = lax.axis_size("dp")
    if size > DIRECT_LIMIT or size & (size - 1):
        return [lax.psum(part, "dp")]
    if size == 1:
        return [part]
    pair = part + lax.ppermute(part, "dp", [(index, index ^ 1) for index in range(size)])
    if beside is not None:
        pair = lax.optimization_barrier((pair, beside))[0]
    parts = [pair]
    offsets = list(range(2, size, 2))
    for offset in offsets[:1] + offsets[:0:-1]:
        parts.append(lax.ppermute(pair, "dp", [(index, index ^ offset) for index in range(size)]))
    return parts


def scale_rows(plan, held, row_scale):
    size = plan.wide[0] * plan.wide[1]
    return pl.pallas_call(
        functools.partial(scale_kernel, plan),
        in_specs=[WHOLE] * 2,
        out_specs=WHOLE,
        out_shape=VM(plan.wide, jnp.float32),
        compiler_params=PARAMS,
        cost_estimate=pl.CostEstimate(flops=2 * size, bytes_accessed=6 * size, transcendentals=0),
        name="scale",
    )(held, row_scale)


def shards(q_grad, k_grad, v_grad, o_grad):
    grads = (q_grad, k_grad, v_grad, o_grad)
    plan = Plan(grads)
    count = plan.count
    f32 = jnp.float32
    row_out = VM(plan.row_shape, f32)
    col_out = VM(plan.col_shape, f32)

    loaded = pl.pallas_call(
        functools.partial(load_kernel, plan),
        in_specs=[OUTSIDE] * count,
        out_specs=[WHOLE] * (count + 2),
        out_shape=[VM(plan.wide, grads[0].dtype)]
        + [VM(grad.shape, f32) for grad in grads]
        + [row_out],
        scratch_shapes=[pltpu.SemaphoreType.DMA((plan.chunks,))],
        compiler_params=PARAMS,
        name="load",
    )(*[pltpu.with_memory_space_constraint(grad, pltpu.HBM) for grad in grads])
    held, squares, row_part = loaded[0], loaded[1 : 1 + count], loaded[1 + count]

    row_scale = col_scale = None
    for sweep in range(ITERS):
        parts = exchange_rows(row_part)
        previous = [] if row_scale is None else [row_scale]
        row_scale, col_part = pl.pallas_call(
            functools.partial(col_kernel, plan, len(parts), bool(previous)),
            in_specs=[WHOLE] * (count + len(parts) + len(previous)),
            out_specs=[WHOLE] * 2,
            out_shape=[row_out, col_out],
            scratch_shapes=[
                VM(plan.row_shape, f32),
                VM((plan.col_shape[0], 8, LANES), f32),
            ],
            compiler_params=PARAMS,
            name=f"col{sweep}",
        )(*squares, *parts, *previous)
        scaled = scale_rows(plan, held, row_scale) if sweep + 1 == ITERS else None
        parts = exchange_cols(col_part, scaled)
        previous = [] if col_scale is None else [col_scale]
        if sweep + 1 == ITERS:
            break
        col_scale, row_part = pl.pallas_call(
            functools.partial(row_kernel, plan, len(parts), bool(previous)),
            in_specs=[WHOLE] * (count + len(parts) + len(previous)),
            out_specs=[WHOLE] * 2,
            out_shape=[col_out, row_out],
            scratch_shapes=[VM(plan.col_shape, f32)],
            compiler_params=PARAMS,
            name=f"row{sweep}",
        )(*squares, *parts, *previous)

    return tuple(
        pl.pallas_call(
            functools.partial(last_kernel, plan, len(parts)),
            in_specs=[WHOLE] * (len(parts) + 2),
            out_specs=[OUTSIDE] * count,
            out_shape=[jax.ShapeDtypeStruct(grad.shape, grad.dtype) for grad in grads],
            scratch_shapes=[VM(plan.col_shape, f32)]
            + [VM(plan.wide, grads[0].dtype)]
            + [pltpu.SemaphoreType.DMA((plan.chunks,))],
            compiler_params=PARAMS,
            name="last",
        )(scaled, *parts, col_scale)
    )


def solution(mesh):
    return jax.shard_map(
        shards,
        mesh=mesh,
        in_specs=(P("dp", "mp"), P("dp", "mp"), P("dp", "mp"), P("dp", "mp")),
        out_specs=(P("dp", "mp"), P("dp", "mp"), P("dp", "mp"), P("dp", "mp")),
        check_vma=False,
    )
```
